1024 devices in a mesh: dp: 64 (over z_hi, x, core), seq: 16 (over z_lo, y).
Axes of the slice: x: 8, y: 8, z: 8 (z_hi: 4, z_lo: 2; z = z_hi * 2 + z_lo), core: 2. Of those that a mesh axis runs over, the one named last changes fastest.
Arguments:
- qkv: bfloat16 [131072, 3, 1152], P(('dp', 'seq')), may hold values from -6 to 6
- attn_out: bfloat16 [131072, 1152], P(('dp', 'seq')), may hold values from -24 to 24
- dout: bfloat16 [131072, 1152], P(('dp', 'seq')), may hold values from -16 to 16
- w_master: float32 [1152, 1152], P('dp', 'seq'), may hold values from -0.1875 to 0.1875
- mom1: float32 [1152, 1152], P('dp', 'seq'), may hold values from -6 to 6
- mom2: float32 [1152, 1152], P('dp', 'seq'), may hold values from 0.5 to 50
- grad_prev: float32 [1152, 1152], P('dp', 'seq'), may hold values from -16 to 16
Outputs:
- dqkv: bfloat16 [131072, 3, 1152], P(('dp', 'seq'))
- grad_new: float32 [1152, 1152], P('dp', 'seq')
- weight_new: float32 [1152, 1152], P('dp', 'seq')
- moment_one: float32 [1152, 1152], P('dp', 'seq')
- moment_two: float32 [1152, 1152], P('dp', 'seq')
The draws below stay inside these ranges and needn't reach their ends.
All inputs are finite; a program needn't handle non-finite values.
Results may differ from the reference program's by a relative error of at most 0.02.
Values may be sent and summed in bfloat16 or wider, within the bound.
No kernel may reach another device: no remote copies, remote signals or barrier semaphores. Data moves between devices by JAX's collectives and lax.ppermute only.
A program may use at most 64 MiB of HBM per device.

```python
import math
import jax
import jax.numpy as jnp
from jax import lax

D = 1152
HEADS = 16
HD = 72
TOK_DEV = 128
TOKENS = 131072
N_DP = 64
N_SEQ = 16


def draw_qkv(key, part):
    first = jax.random.fold_in(key, 0)
    values = jax.random.truncated_normal(first, -6.0, 6.0, (TOKENS, 3, D), jnp.float32)
    return values.astype(jnp.bfloat16)


def spiked(values, stream_key, source, target, parts, factor):
    def block_of(position):
        return (jnp.arange(values.shape[position]) // (values.shape[position] // parts)).reshape((-1,) + (1,) * (values.ndim - 1 - position))

    first = jax.random.permutation(stream_key, parts)[block_of(target)]
    far = (block_of(target) + parts // 2) % parts
    return jnp.where((block_of(source) == first) | (block_of(source) == far), factor * values, values)


def block_scale(key, extent, cuts, least, largest):
    def one(dim, blocks):
        heights = jax.random.uniform(jax.random.fold_in(jax.random.fold_in(key, 6), dim), (blocks,), jnp.float32, least / len(cuts), largest / len(cuts))
        return jnp.repeat(jnp.exp(heights), extent[dim] // blocks).reshape((-1,) + (1,) * (len(extent) - dim - 1))

    gain = one(*cuts[0])
    for cut in cuts[1:]:
        gain = gain * one(*cut)
    return gain


def noise(stream_key, shape, spread, most, cuts=(), kind=jnp.bfloat16):
    values = jax.random.normal(stream_key, shape, jnp.float32) * spread
    if len(cuts) > 0:
        values = block_scale(stream_key, shape, cuts, -0.22, 0.18) * values
    return jnp.clip(values, min=-most, max=most).astype(kind)


def bell_draw_with(key, dims, width, reach, pieces, heavy, held_as=jnp.bfloat16):
    array = width * jax.random.normal(key, dims, jnp.float32)
    if pieces:
        array = array * block_scale(key, dims, pieces, -0.22, 0.18)
    return jnp.clip(spiked(array, jax.random.fold_in(key, 3), *heavy), -reach, reach).astype(held_as)


def setup_inputs(seed: int = 0) -> dict:
    seeds = jax.random.split(jax.random.key(seed), 8)
    qkv = draw_qkv(jax.random.fold_in(seeds[7], 71), 0)
    attn_out = bell_draw_with(seeds[1], (TOKENS, D), 1.0, 24.0, ((0, 1024),), (0, 1, 128, 5.5))
    dout = noise(seeds[2], (TOKENS, D), 4.0, 16.0, ((0, 1024),))
    w_master = noise(seeds[3], (D, D), D ** -0.5, 0.1875, ((0, 64), (1, 16)), jnp.float32)
    mom1 = noise(seeds[4], (D, D), 1.0, 6.0, ((0, 64), (1, 16)), jnp.float32)
    mom2 = jnp.clip(jnp.exp(math.log(50.0) - 4.6051702 * jax.random.uniform(seeds[5], (D, D), jnp.float32) ** block_scale(seeds[5], (D, D), ((0, 64), (1, 16)), -0.2, 0.2)), 0.5, 50.0)
    grad_prev = noise(seeds[6], (D, D), 4.0, 16.0, ((0, 64), (1, 16)), jnp.float32)
    return {"qkv": qkv, "attn_out": attn_out, "dout": dout, "w_master": w_master, "mom1": mom1, "mom2": mom2, "grad_prev": grad_prev}


BETA_ONE = 0.9
BETA_TWO = 0.999
LEARN_RATE = 0.001
ADAM_EPS = 1e-08
CORRECT_ONE = 0.999973438601112
CORRECT_TWO = 0.0952078528862904

def head_backward(queries, key_rows, value_rows, grad_rows):
    factor = HD ** (-0.5)
    scores = jnp.dot(queries, key_rows.T, preferred_element_type=jnp.float32) * factor
    row_max = lax.optimization_barrier(jnp.max(scores, axis=-1, keepdims=True))
    exponent = jnp.exp(scores - row_max)
    attention = exponent / lax.optimization_barrier(jnp.sum(exponent, axis=-1, keepdims=True))
    attn_half = attention.astype(jnp.bfloat16)
    grad_probs = jnp.dot(grad_rows, value_rows.T, preferred_element_type=jnp.float32)
    row_dot = lax.optimization_barrier(jnp.sum(attention * grad_probs, axis=-1, keepdims=True))
    grad_logits = (attention * (grad_probs - row_dot) * factor).astype(jnp.bfloat16)
    grad_query = jnp.dot(grad_logits, key_rows, preferred_element_type=jnp.float32).astype(jnp.bfloat16)
    grad_keys = jnp.dot(grad_logits.T, queries, preferred_element_type=jnp.float32).astype(jnp.bfloat16)
    grad_values = jnp.dot(attn_half.T, grad_rows, preferred_element_type=jnp.float32).astype(jnp.bfloat16)
    return jnp.stack([grad_query, grad_keys, grad_values], axis=1)

def reference(qkv, attn_out, dout, w_master, mom1, mom2, grad_prev):
    moment_one = BETA_ONE * mom1 + (1.0 - BETA_ONE) * grad_prev
    moment_two = BETA_TWO * mom2 + (1.0 - BETA_TWO) * grad_prev * grad_prev
    weight_new = w_master - LEARN_RATE * (moment_one / CORRECT_ONE) / (jnp.sqrt(moment_two / CORRECT_TWO) + ADAM_EPS)
    weight_half = weight_new.astype(jnp.bfloat16)
    attn_grad = lax.dot_general(dout, weight_half, (((1,), (1,)), ((), ())), preferred_element_type=jnp.float32).astype(jnp.bfloat16)
    seq_len = TOK_DEV * N_SEQ
    clip_count = TOKENS // seq_len
    clip_qkv = qkv.reshape(clip_count, seq_len, 3, HEADS, HD)
    clip_grad = attn_grad.reshape(clip_count, seq_len, HEADS, HD)

    def one_head(operands):
        head_qkv, head_grad = operands
        return head_backward(head_qkv[:, 0], head_qkv[:, 1], head_qkv[:, 2], head_grad)

    def one_clip(operands):
        part_qkv, part_grad = operands
        heads_qkv = jnp.moveaxis(part_qkv, 2, 0)
        heads_grad = jnp.moveaxis(part_grad, 1, 0)
        result = lax.map(one_head, (heads_qkv, heads_grad))
        return jnp.moveaxis(result, 0, 2)
    dqkv = lax.map(one_clip, (clip_qkv, clip_grad)).reshape(TOKENS, 3, D)
    factor = float(TOKENS) ** (-0.5)
    out_blocks = attn_out.reshape(N_DP, N_SEQ, TOK_DEV, D)
    dout_blocks = dout.reshape(N_DP, N_SEQ, TOK_DEV, D)

    def add_device(carry, operands):
        out_rows, dout_rows = operands
        term = jnp.dot(out_rows.T, dout_rows, preferred_element_type=jnp.float32) * factor
        rounded = lax.optimization_barrier(term.astype(jnp.bfloat16)).astype(jnp.float32)
        return (carry + rounded, None)

    def add_group(carry, operands):
        group_out, group_dout = operands
        group_sum, unused = lax.scan(add_device, jnp.zeros((D, D), jnp.float32), (group_out, group_dout))
        return (carry + group_sum, None)
    grad_new, unused = lax.scan(add_group, jnp.zeros((D, D), jnp.float32), (out_blocks, dout_blocks))
    return (dqkv, grad_new, weight_new, moment_one, moment_two)
```

```python
import jax
import jax.numpy as jnp
from jax import lax
from jax.experimental import pallas as pl
from jax.experimental.pallas import tpu as pltpu
from jax.sharding import Mesh, PartitionSpec as P

HD = 72
BLOCK = 256

BETA_ONE = 0.9
BETA_TWO = 0.999
LEARN_RATE = 0.001
ADAM_EPS = 1e-08
CORRECT_ONE = 0.999973438601112
CORRECT_TWO = 0.0952078528862904
LOG2_E = 1.4426950408889634


def probs_kernel(heads_ref, probs_ref, keys_ref):
    blocks = heads_ref.shape[0]
    width = heads_ref.shape[3]
    step = pl.program_id(0)

    @pl.when(step == 0)
    def _():
        for s in range(blocks):
            keys_ref[s * width : (s + 1) * width, :] = heads_ref[s, 1].T

    per = probs_ref.shape[1] // width
    queries = jnp.concatenate([heads_ref[step * per + j, 0] for j in range(per)], axis=1)
    scores = lax.dot_general(
        keys_ref[...], queries, (((1,), (0,)), ((), ())), preferred_element_type=jnp.float32
    )
    top = jnp.max(scores, axis=0, keepdims=True)
    weights = jnp.exp2((scores - top) * (HD ** (-0.5) * LOG2_E))
    total = jnp.sum(weights, axis=0, keepdims=True)
    probs_ref[...] = (weights * (1.0 / total)).astype(jnp.bfloat16)


def grads_kernel(
    heads_ref, grad_ref, probs_ref, out_ref, keys_ref, values_ref, grads_ref, dkeys_ref, dvalues_ref
):
    blocks = heads_ref.shape[0]
    width = heads_ref.shape[3]
    step = pl.program_id(0)
    per = probs_ref.shape[1] // width
    block = per * width
    factor = HD ** (-0.5)

    @pl.when(step == 0)
    def _():
        for s in range(blocks):
            keys_ref[:, s * width : (s + 1) * width] = heads_ref[s, 1]
            values_ref[s * width : (s + 1) * width, :] = heads_ref[s, 2].T
        dkeys_ref[...] = jnp.zeros_like(dkeys_ref)
        dvalues_ref[...] = jnp.zeros_like(dvalues_ref)
        count = HD // 2
        stride = grad_ref.shape[1] // 2
        dims = lax.broadcasted_iota(jnp.int32, (HD, stride), 0)
        order = lax.broadcasted_iota(jnp.int32, (HD, stride), 1)
        run = jnp.zeros_like(order)
        for k in range(1, count // SHARE):
            run += (order >= k * SHARE).astype(jnp.int32)
        side = blocks // 2
        parts = []
        for h in range(2):
            pieces = []
            for s in range(blocks):
                start = (h ^ (s // side)) * stride
                pieces.append(grad_ref[h * side + s % side, start : start + stride, :])
            choose = ((dims == order + SHARE * (run + h)) & (order < count)).astype(jnp.bfloat16)
            parts.append(
                lax.dot_general(
                    choose,
                    jnp.concatenate(pieces, axis=1),
                    (((1,), (0,)), ((), ())),
                    preferred_element_type=jnp.float32,
                )
            )
        placed = (parts[0] + parts[1]).astype(jnp.bfloat16)
        for b in range(pl.cdiv(blocks, per)):
            grads_ref[b] = placed[:, b * block : (b + 1) * block]

    grads_t = grads_ref[step]
    queries = jnp.concatenate([heads_ref[step * per + j, 0].T for j in range(per)], axis=0)
    half = probs_ref[...]
    grad_probs = lax.dot_general(
        values_ref[...], grads_t, (((1,), (0,)), ((), ())), preferred_element_type=jnp.float32
    )
    probs = half.astype(jnp.float32)
    row_dot = jnp.sum(probs * grad_probs, axis=0, keepdims=True)
    logits = (probs * (grad_probs - row_dot)).astype(jnp.bfloat16)
    dvalues_ref[...] += lax.dot_general(
        half, grads_t.T, (((1,), (0,)), ((), ())), preferred_element_type=jnp.float32
    )
    dkeys_ref[...] += lax.dot_general(
        logits, queries, (((1,), (0,)), ((), ())), preferred_element_type=jnp.float32
    )
    dqueries = factor * lax.dot_general(
        keys_ref[...], logits, (((1,), (0,)), ((), ())), preferred_element_type=jnp.float32
    )
    for j in range(per):
        out_ref[step * per + j, 0] = dqueries[:, j * width : (j + 1) * width].astype(jnp.bfloat16)

    @pl.when(step == pl.num_programs(0) - 1)
    def _():
        for s in range(blocks):
            out_ref[s, 1] = (dkeys_ref[s * width : (s + 1) * width, :].T * factor).astype(jnp.bfloat16)
            out_ref[s, 2] = dvalues_ref[s * width : (s + 1) * width, :].T.astype(jnp.bfloat16)


def whole(shape):
    return pl.BlockSpec(shape, lambda i: (0,) * len(shape))


def probs_call(heads):
    count, _, dims, width = heads.shape
    length = count * width
    block = min(BLOCK, length)
    return pl.pallas_call(
        probs_kernel,
        out_shape=jax.ShapeDtypeStruct((length, length), jnp.bfloat16),
        grid=(length // block,),
        in_specs=[whole(heads.shape)],
        out_specs=pl.BlockSpec((length, block), lambda i: (0, i)),
        scratch_shapes=[pltpu.VMEM((length, dims), jnp.bfloat16)],
        compiler_params=pltpu.CompilerParams(vmem_limit_bytes=48 * 2**20),
        cost_estimate=pl.CostEstimate(
            flops=2 * length * length * 256, transcendentals=length * length, bytes_accessed=2 * length * length
        ),
        name="probs",
    )(heads)


def grads_call(heads, grad, probs):
    count, _, dims, width = heads.shape
    length = count * width
    block = min(BLOCK, length)
    return pl.pallas_call(
        grads_kernel,
        out_shape=jax.ShapeDtypeStruct(heads.shape, jnp.bfloat16),
        grid=(length // block,),
        in_specs=[whole(heads.shape), whole(grad.shape), pl.BlockSpec((length, block), lambda i: (0, i))],
        out_specs=whole(heads.shape),
        scratch_shapes=[
            pltpu.VMEM((dims, length), jnp.bfloat16),
            pltpu.VMEM((length, dims), jnp.bfloat16),
            pltpu.VMEM((length // block, dims, block), jnp.bfloat16),
            pltpu.VMEM((length, dims), jnp.float32),
            pltpu.VMEM((length, dims), jnp.float32),
        ],
        compiler_params=pltpu.CompilerParams(vmem_limit_bytes=48 * 2**20),
        cost_estimate=pl.CostEstimate(
            flops=8 * length * length * 256, transcendentals=0, bytes_accessed=2 * length * length
        ),
        name="grads",
    )(heads, grad, probs)


def term_kernel(core_ref, dout_ref, out_in_ref, kept_ref, sent_ref, *, factor):
    half = out_in_ref.shape[1] // 2
    turned = dout_ref[...].T
    for side in range(2):
        product = lax.dot_general(
            turned,
            out_in_ref[:, side * half : (side + 1) * half],
            (((1,), (0,)), ((), ())),
            preferred_element_type=jnp.float32,
        )
        rounded = (product * factor).astype(jnp.bfloat16)
        if side == 0:
            kept_ref[:, half:] = jnp.zeros_like(kept_ref[:, half:])
            sent_ref[:, half:] = jnp.zeros_like(sent_ref[:, half:])

        @pl.when(core_ref[0] == side)
        def _():
            kept_ref[:, :half] = rounded

        @pl.when(core_ref[0] != side)
        def _():
            sent_ref[:, :half] = rounded


def term_call(core, dout, attn_out, factor):
    tokens, width = dout.shape
    kind = jax.ShapeDtypeStruct((width, pl.cdiv(width // 2, LANES) * LANES), jnp.bfloat16)
    vmem = pl.BlockSpec(memory_space=pltpu.VMEM)
    return pl.pallas_call(
        lambda *refs: term_kernel(*refs, factor=factor),
        out_shape=(kind, kind),
        in_specs=[pl.BlockSpec(memory_space=pltpu.SMEM), vmem, vmem],
        out_specs=(vmem, vmem),
        compiler_params=pltpu.CompilerParams(vmem_limit_bytes=32 * 2**20),
        cost_estimate=pl.CostEstimate(
            flops=2 * width * width * 256, transcendentals=0, bytes_accessed=2 * width * width
        ),
        name="term",
    )(core, dout, attn_out)


def project_kernel(core_ref, own_ref, other_ref, dout_ref, near_ref, out_ref, rows_ref):
    blocks = out_ref.shape[0] * 2
    width = dout_ref.shape[0]
    count = rows_ref.shape[2]
    tokens = jnp.concatenate([dout_ref[...], near_ref[...]], axis=0)
    for source, flip in ((own_ref, 0), (other_ref, 1)):
        product = lax.dot_general(
            source[...], tokens, (((1,), (1,)), ((), ())), preferred_element_type=jnp.float32
        )
        for parity in range(2):

            @pl.when(core_ref[0] == parity ^ flip)
            def _():
                for b in range(blocks):
                    start = ((b % 2) * 2 + parity) * SHARE
                    for side in range(2):
                        rows_ref[b // 2, side, start : start + SHARE, :] = product[
                            b * SHARE : (b + 1) * SHARE, side * width : (side + 1) * width
                        ]

    stride = out_ref.shape[1] // 2
    for side in range(2):
        out_ref[:, side * stride : side * stride + count, :] = rows_ref[:, side].astype(jnp.bfloat16)
        out_ref[:, side * stride + count : (side + 1) * stride, :] = jnp.zeros(
            (blocks // 2, stride - count, width), jnp.bfloat16
        )


def project_call(core, own, other, dout, near, heads):
    tokens, width = dout.shape
    count = 2 * own.shape[0] // heads
    shape = (heads, 2 * (pl.cdiv(count, 8) * 8), tokens)
    vmem = pl.BlockSpec(memory_space=pltpu.VMEM)
    return pl.pallas_call(
        project_kernel,
        out_shape=jax.ShapeDtypeStruct(shape, jnp.bfloat16),
        in_specs=[pl.BlockSpec(memory_space=pltpu.SMEM), vmem, vmem, vmem, vmem],
        out_specs=vmem,
        scratch_shapes=[pltpu.VMEM((heads, 2, count, tokens), jnp.float32)],
        compiler_params=pltpu.CompilerParams(vmem_limit_bytes=32 * 2**20),
        cost_estimate=pl.CostEstimate(
            flops=4 * width * width * tokens, transcendentals=0, bytes_accessed=4 * width * width
        ),
        name="project",
    )(core, own, other, dout, near)


SEQ = ("zl", "y")
ROWS = ("zh", "x")
DP = ("zh", "x", "c")
SHARE = 9
LANES = 128
SWAP = [(0, 1), (1, 0)]


def exchange(array, axes):
    return lax.all_to_all(array, axes, 0, 0, tiled=True)


def per_device(qkv, attn_out, dout, w_master, mom1, mom2, grad_prev):
    tokens, _, width = qkv.shape
    seq_count = lax.axis_size(SEQ)
    row_count = lax.axis_size(ROWS)
    rows, cols = w_master.shape
    core = lax.axis_index("c")
    core_id = core[None].astype(jnp.int32)

    moment_one = BETA_ONE * mom1 + (1.0 - BETA_ONE) * grad_prev
    moment_two = BETA_TWO * mom2 + (1.0 - BETA_TWO) * grad_prev * grad_prev
    weight_new = w_master - LEARN_RATE * (moment_one / CORRECT_ONE) / (
        jnp.sqrt(moment_two / CORRECT_TWO) + ADAM_EPS
    )
    weight_half = weight_new.astype(jnp.bfloat16)

    by_head = jnp.transpose(qkv.reshape(tokens, 3, seq_count, HD), (2, 1, 3, 0)).reshape(seq_count, 3 * HD, tokens)
    size = SHARE * cols
    flat = jnp.pad(weight_half.reshape(2, size), ((0, 0), (0, 8 * LANES - size))).reshape(2, 1, 8, LANES)
    flat = jnp.broadcast_to(flat, (2, seq_count // 2, 8, LANES)).reshape(seq_count, 8, LANES)
    packed = jnp.concatenate([by_head, flat], axis=1)
    packed, dout, attn_out = lax.optimization_barrier((packed, dout, attn_out))
    near = lax.ppermute(dout, "zl", SWAP)
    arrived = exchange(packed, SEQ)
    heads_qkv = arrived[:, : 3 * HD].reshape(seq_count, 3, HD, tokens)
    columns = arrived[:, 3 * HD :].reshape(seq_count, 8 * LANES)[:, :size].reshape(seq_count, SHARE, cols)

    factor = float(tokens * seq_count * lax.axis_size(DP)) ** (-0.5)
    kept, sent = term_call(core_id, dout, attn_out, factor)
    sent = lax.ppermute(sent, "c", SWAP)
    pair = (kept.astype(jnp.float32) + sent.astype(jnp.float32)).astype(jnp.bfloat16)

    row_block = jnp.transpose(columns, (1, 0, 2)).reshape(SHARE * width // LANES, LANES)
    row_block, pair, near = lax.optimization_barrier((row_block, pair, near))
    own = exchange(jnp.broadcast_to(row_block[None], (row_count,) + row_block.shape), ROWS)
    probs = probs_call(heads_qkv)
    own, probs = lax.optimization_barrier((own, probs))
    own = own.reshape(row_count * SHARE, width)
    other = lax.ppermute(own, "c", SWAP)
    grad_rows = project_call(core_id, own, other, dout, near, seq_count)
    heads_grad = exchange(grad_rows, SEQ)

    clip = lax.psum_scatter(pair, SEQ, scatter_dimension=0, tiled=True)
    clip, heads_grad = lax.optimization_barrier((clip, heads_grad))
    line, across = lax.axis_size("x"), lax.axis_size("zh")
    pieces = jnp.transpose(clip[:, : width // 2].T.reshape(across, line, rows * cols), (1, 0, 2))
    pieces = jnp.sum(exchange(pieces, "x").astype(jnp.float32), axis=0)
    grad_new = jnp.zeros((rows * cols,), jnp.float32)
    for turn in range(across):
        moves = [
            ((z * line + x) * 2 + c, (c * across + (z + turn) % across) * line + x)
            for z in range(across)
            for x in range(line)
            for c in range(2)
        ]
        piece = lax.dynamic_slice_in_dim(pieces, (lax.axis_index("zh") + turn) % across, 1, 0)[0]
        grad_new = grad_new + lax.ppermute(piece, DP, moves)
    grad_new = grad_new.reshape(rows, cols)

    local = grads_call(heads_qkv, heads_grad, probs)
    back = exchange(local, SEQ)
    dqkv = jnp.transpose(back, (3, 1, 0, 2)).reshape(tokens, 3, width)
    return (dqkv, grad_new, weight_new, moment_one, moment_two)


def solution(mesh):
    fine = Mesh(mesh.devices.reshape(4, 8, 2, 2, 8), ("zh", "x", "c", "zl", "y"))
    rows = P(DP + SEQ)
    square = P(DP, SEQ)
    return jax.shard_map(
        per_device,
        mesh=fine,
        in_specs=(rows, rows, rows, square, square, square, square),
        out_specs=(rows, square, square, square, square),
        check_vma=False,
    )
```

```python
import math

import jax
import jax.numpy as jnp
from jax import lax
from jax.experimental import pallas as pl
from jax.experimental.pallas import tpu as pltpu
from jax.sharding import Mesh, PartitionSpec as P

HD = 72
BLOCK = 256

BETA_ONE = 0.9
BETA_TWO = 0.999
LEARN_RATE = 0.001
ADAM_EPS = 1e-08
CORRECT_ONE = 0.999973438601112
CORRECT_TWO = 0.0952078528862904
LOG2_E = 1.4426950408889634


def probs_kernel(heads_ref, probs_ref, keys_ref):
    blocks = heads_ref.shape[0]
    width = heads_ref.shape[3]
    step = pl.program_id(0)

    @pl.when(step == 0)
    def _():
        for s in range(blocks):
            keys_ref[s * width : (s + 1) * width, :] = heads_ref[s, 1].T

    per = probs_ref.shape[1] // width
    queries = jnp.concatenate([heads_ref[step * per + j, 0] for j in range(per)], axis=1)
    scores = lax.dot_general(
        keys_ref[...], queries, (((1,), (0,)), ((), ())), preferred_element_type=jnp.float32
    )
    top = jnp.max(scores, axis=0, keepdims=True)
    weights = jnp.exp2((scores - top) * (HD ** (-0.5) * LOG2_E))
    total = jnp.sum(weights, axis=0, keepdims=True)
    probs_ref[...] = (weights * (1.0 / total)).astype(jnp.bfloat16)


def grads_kernel(
    heads_ref, grad_ref, probs_ref, out_ref, keys_ref, values_ref, grads_ref, dkeys_ref, dvalues_ref
):
    blocks = heads_ref.shape[0]
    width = heads_ref.shape[3]
    step = pl.program_id(0)
    per = probs_ref.shape[1] // width
    block = per * width
    factor = HD ** (-0.5)

    @pl.when(step == 0)
    def _():
        for s in range(blocks):
            keys_ref[:, s * width : (s + 1) * width] = heads_ref[s, 1]
            values_ref[s * width : (s + 1) * width, :] = heads_ref[s, 2].T
        dkeys_ref[...] = jnp.zeros_like(dkeys_ref)
        dvalues_ref[...] = jnp.zeros_like(dvalues_ref)
        count = HD // 2
        stride = grad_ref.shape[1] // 2
        dims = lax.broadcasted_iota(jnp.int32, (HD, stride), 0)
        order = lax.broadcasted_iota(jnp.int32, (HD, stride), 1)
        run = jnp.zeros_like(order)
        for k in range(1, count // SHARE):
            run += (order >= k * SHARE).astype(jnp.int32)
        side = blocks // 2
        parts = []
        for h in range(2):
            pieces = []
            for s in range(blocks):
                start = (h ^ (s // side)) * stride
                pieces.append(grad_ref[h * side + s % side, start : start + stride, :])
            choose = ((dims == order + SHARE * (run + h)) & (order < count)).astype(jnp.bfloat16)
            parts.append(
                lax.dot_general(
                    choose,
                    jnp.concatenate(pieces, axis=1),
                    (((1,), (0,)), ((), ())),
                    preferred_element_type=jnp.float32,
                )
            )
        placed = (parts[0] + parts[1]).astype(jnp.bfloat16)
        for b in range(pl.cdiv(blocks, per)):
            grads_ref[b] = placed[:, b * block : (b + 1) * block]

    grads_t = grads_ref[step]
    queries = jnp.concatenate([heads_ref[step * per + j, 0].T for j in range(per)], axis=0)
    half = probs_ref[...]
    grad_probs = lax.dot_general(
        values_ref[...], grads_t, (((1,), (0,)), ((), ())), preferred_element_type=jnp.float32
    )
    probs = half.astype(jnp.float32)
    row_dot = jnp.sum(probs * grad_probs, axis=0, keepdims=True)
    logits = (probs * (grad_probs - row_dot)).astype(jnp.bfloat16)
    dvalues_ref[...] += lax.dot_general(
        half, grads_t.T, (((1,), (0,)), ((), ())), preferred_element_type=jnp.float32
    )
    dkeys_ref[...] += lax.dot_general(
        logits, queries, (((1,), (0,)), ((), ())), preferred_element_type=jnp.float32
    )
    dqueries = factor * lax.dot_general(
        keys_ref[...], logits, (((1,), (0,)), ((), ())), preferred_element_type=jnp.float32
    )
    for j in range(per):
        out_ref[step * per + j, 0] = dqueries[:, j * width : (j + 1) * width].astype(jnp.bfloat16)

    @pl.when(step == pl.num_programs(0) - 1)
    def _():
        for s in range(blocks):
            out_ref[s, 1] = (dkeys_ref[s * width : (s + 1) * width, :].T * factor).astype(jnp.bfloat16)
            out_ref[s, 2] = dvalues_ref[s * width : (s + 1) * width, :].T.astype(jnp.bfloat16)


def whole(shape):
    return pl.BlockSpec(shape, lambda i: (0,) * len(shape))


def probs_call(heads):
    count, _, dims, width = heads.shape
    length = count * width
    block = min(BLOCK, length)
    return pl.pallas_call(
        probs_kernel,
        out_shape=jax.ShapeDtypeStruct((length, length), jnp.bfloat16),
        grid=(length // block,),
        in_specs=[whole(heads.shape)],
        out_specs=pl.BlockSpec((length, block), lambda i: (0, i)),
        scratch_shapes=[pltpu.VMEM((length, dims), jnp.bfloat16)],
        compiler_params=pltpu.CompilerParams(vmem_limit_bytes=48 * 2**20),
        cost_estimate=pl.CostEstimate(
            flops=2 * length * length * 256, transcendentals=length * length, bytes_accessed=2 * length * length
        ),
        name="probs",
    )(heads)


def grads_call(heads, grad, probs):
    count, _, dims, width = heads.shape
    length = count * width
    block = min(BLOCK, length)
    return pl.pallas_call(
        grads_kernel,
        out_shape=jax.ShapeDtypeStruct(heads.shape, jnp.bfloat16),
        grid=(length // block,),
        in_specs=[whole(heads.shape), whole(grad.shape), pl.BlockSpec((length, block), lambda i: (0, i))],
        out_specs=whole(heads.shape),
        scratch_shapes=[
            pltpu.VMEM((dims, length), jnp.bfloat16),
            pltpu.VMEM((length, dims), jnp.bfloat16),
            pltpu.VMEM((length // block, dims, block), jnp.bfloat16),
            pltpu.VMEM((length, dims), jnp.float32),
            pltpu.VMEM((length, dims), jnp.float32),
        ],
        compiler_params=pltpu.CompilerParams(vmem_limit_bytes=48 * 2**20),
        cost_estimate=pl.CostEstimate(
            flops=8 * length * length * 256, transcendentals=0, bytes_accessed=2 * length * length
        ),
        name="grads",
    )(heads, grad, probs)


def term_kernel(core_ref, dout_ref, out_in_ref, kept_ref, sent_ref, *, factor):
    half = out_in_ref.shape[1] // 2
    turned = dout_ref[...].T
    for side in range(2):
        product = lax.dot_general(
            turned,
            out_in_ref[:, side * half : (side + 1) * half],
            (((1,), (0,)), ((), ())),
            preferred_element_type=jnp.float32,
        )
        rounded = (product * factor).astype(jnp.bfloat16)
        if side == 0:
            kept_ref[:, half:] = jnp.zeros_like(kept_ref[:, half:])
            sent_ref[:, half:] = jnp.zeros_like(sent_ref[:, half:])

        @pl.when(core_ref[0] == side)
        def _():
            kept_ref[:, :half] = rounded

        @pl.when(core_ref[0] != side)
        def _():
            sent_ref[:, :half] = rounded


def term_call(core, dout, attn_out, factor):
    tokens, width = dout.shape
    kind = jax.ShapeDtypeStruct((width, pl.cdiv(width // 2, LANES) * LANES), jnp.bfloat16)
    vmem = pl.BlockSpec(memory_space=pltpu.VMEM)
    return pl.pallas_call(
        lambda *refs: term_kernel(*refs, factor=factor),
        out_shape=(kind, kind),
        in_specs=[pl.BlockSpec(memory_space=pltpu.SMEM), vmem, vmem],
        out_specs=(vmem, vmem),
        compiler_params=pltpu.CompilerParams(vmem_limit_bytes=32 * 2**20),
        cost_estimate=pl.CostEstimate(
            flops=2 * width * width * 256, transcendentals=0, bytes_accessed=2 * width * width
        ),
        name="term",
    )(core, dout, attn_out)


def project_kernel(core_ref, own_ref, other_ref, dout_ref, near_ref, out_ref, rows_ref):
    blocks = out_ref.shape[0] * 2
    width = dout_ref.shape[0]
    count = rows_ref.shape[2]
    tokens = jnp.concatenate([dout_ref[...], near_ref[...]], axis=0)
    for source, flip in ((own_ref, 0), (other_ref, 1)):
        product = lax.dot_general(
            source[...], tokens, (((1,), (1,)), ((), ())), preferred_element_type=jnp.float32
        )
        for parity in range(2):

            @pl.when(core_ref[0] == parity ^ flip)
            def _():
                for b in range(blocks):
                    start = ((b % 2) * 2 + parity) * SHARE
                    for side in range(2):
                        rows_ref[b // 2, side, start : start + SHARE, :] = product[
                            b * SHARE : (b + 1) * SHARE, side * width : (side + 1) * width
                        ]

    stride = out_ref.shape[1] // 2
    for side in range(2):
        out_ref[:, side * stride : side * stride + count, :] = rows_ref[:, side].astype(jnp.bfloat16)
        out_ref[:, side * stride + count : (side + 1) * stride, :] = jnp.zeros(
            (blocks // 2, stride - count, width), jnp.bfloat16
        )


def project_call(core, own, other, dout, near, heads):
    tokens, width = dout.shape
    count = 2 * own.shape[0] // heads
    shape = (heads, 2 * (pl.cdiv(count, 8) * 8), tokens)
    vmem = pl.BlockSpec(memory_space=pltpu.VMEM)
    return pl.pallas_call(
        project_kernel,
        out_shape=jax.ShapeDtypeStruct(shape, jnp.bfloat16),
        in_specs=[pl.BlockSpec(memory_space=pltpu.SMEM), vmem, vmem, vmem, vmem],
        out_specs=vmem,
        scratch_shapes=[pltpu.VMEM((heads, 2, count, tokens), jnp.float32)],
        compiler_params=pltpu.CompilerParams(vmem_limit_bytes=32 * 2**20),
        cost_estimate=pl.CostEstimate(
            flops=4 * width * width * tokens, transcendentals=0, bytes_accessed=4 * width * width
        ),
        name="project",
    )(core, own, other, dout, near)


def pick_kernel(place_ref, heads_ref, near_ref, *out_refs):
    count = len(out_refs)
    for turn in range(count):
        target = (place_ref[1] + turn) % count
        out_refs[turn][0] = heads_ref[place_ref[0] * count + target]
        out_refs[turn][1] = near_ref[target]


def place_kernel(place_ref, *refs):
    in_refs, out_ref = refs[:-1], refs[-1]
    count = len(in_refs)
    for turn in range(count):
        origin = (place_ref[1] + count - turn) % count
        out_ref[place_ref[0] * count + origin] = in_refs[turn][0]
        out_ref[(1 - place_ref[0]) * count + origin] = in_refs[turn][1]


def arrange_kernel(place_ref, clip_ref, *refs):
    out_refs, blocks_ref = refs[:-1], refs[-1]
    line, across, rows = blocks_ref.shape[0], blocks_ref.shape[1], ROWS_DEV
    cols = clip_ref.shape[1]
    total = clip_ref[0].astype(jnp.float32)
    for s in range(1, clip_ref.shape[0]):
        total = total + clip_ref[s].astype(jnp.float32)
    turned = total.T
    blocks_ref[...] = jnp.zeros_like(blocks_ref)
    for z in range(across):
        for x in range(line):
            start = (z * line + x) * rows
            blocks_ref[x, z, :rows, :cols] = turned[start : start + rows]
    for turn in range(line):
        out_refs[turn][...] = blocks_ref[(place_ref[2] + turn) % line]


def gather_kernel(place_ref, *refs):
    total_ref, count = refs[-1], refs[-1].shape[0]
    in_refs, out_refs = refs[: -1 - count], refs[-1 - count : -1]
    total = in_refs[0][...]
    for ref in in_refs[1:]:
        total = total + ref[...]
    total_ref[...] = total
    for turn in range(count):
        out_refs[turn][...] = total_ref[(place_ref[3] + turn) % count]


def moved_call(kernel, name, place, operands, out_shape, scratch=()):
    vmem = pl.BlockSpec(memory_space=pltpu.VMEM)
    size = sum(operand.size for operand in operands)
    return pl.pallas_call(
        kernel,
        out_shape=out_shape,
        in_specs=[pl.BlockSpec(memory_space=pltpu.SMEM)] + [vmem] * len(operands),
        out_specs=jax.tree.map(lambda leaf: vmem, out_shape),
        scratch_shapes=scratch,
        compiler_params=pltpu.CompilerParams(vmem_limit_bytes=16 * 2**20),
        cost_estimate=pl.CostEstimate(flops=0, transcendentals=0, bytes_accessed=0 if scratch else 4 * size),
        name=name,
    )(place, *operands)


SEQ = ("zl", "y")
ROWS = ("zh", "x")
DP = ("zh", "x", "c")
ROWS_DEV = 18
SHARE = 9
LANES = 128
SWAP = [(0, 1), (1, 0)]


def exchange(array, axes):
    return lax.all_to_all(array, axes, 0, 0, tiled=True)


def at(array, index):
    return lax.dynamic_index_in_dim(array, index, 0, keepdims=False)


def per_device(qkv, attn_out, dout, w_master, mom1, mom2, grad_prev):
    tokens, _, width = qkv.shape
    seq_count = lax.axis_size(SEQ)
    row_count = lax.axis_size(ROWS)
    ring = lax.axis_size("y")
    rows, cols = w_master.shape
    core, side, step = lax.axis_index("c"), lax.axis_index("zl"), lax.axis_index("y")
    core_id = core[None].astype(jnp.int32)
    place = jnp.stack([side, step, lax.axis_index("x"), lax.axis_index("zh")]).astype(jnp.int32)

    moment_one = BETA_ONE * mom1 + (1.0 - BETA_ONE) * grad_prev
    moment_two = BETA_TWO * mom2 + (1.0 - BETA_TWO) * grad_prev * grad_prev
    weight_new = w_master - LEARN_RATE * (moment_one / CORRECT_ONE) / (
        jnp.sqrt(moment_two / CORRECT_TWO) + ADAM_EPS
    )
    weight_half = weight_new.astype(jnp.bfloat16)

    size = SHARE * cols
    flat = jnp.pad(weight_half.reshape(2, size), ((0, 0), (0, 8 * LANES - size))).reshape(2, 1, 8, LANES)
    flat = jnp.broadcast_to(flat, (2, seq_count // 2, 8, LANES)).reshape(seq_count, 8, LANES)
    flat, qkv = lax.optimization_barrier((flat, qkv))
    columns = exchange(flat, SEQ).reshape(seq_count, 8 * LANES)[:, :size].reshape(seq_count, SHARE, cols)

    by_head = jnp.transpose(qkv.reshape(tokens, 3, seq_count, HD), (2, 1, 3, 0)).reshape(seq_count, 3 * HD, tokens)
    passed = lax.ppermute(at(by_head.reshape(2, ring, 3 * HD, tokens), 1 - side), "zl", SWAP)
    pair_of = jax.ShapeDtypeStruct((2, 3 * HD, tokens), jnp.bfloat16)
    turns = list(moved_call(pick_kernel, "pick", place, (by_head, passed), (pair_of,) * ring))

    lane = math.gcd(SHARE * width, LANES)
    row_block = jnp.transpose(columns, (1, 0, 2)).reshape(SHARE * width // lane, lane)
    row_block, turns, place = lax.optimization_barrier((row_block, turns, place))
    row_block, dout, attn_out = lax.optimization_barrier((row_block, dout, attn_out))
    near = lax.ppermute(dout, "zl", SWAP)
    own = exchange(jnp.broadcast_to(row_block[None], (row_count,) + row_block.shape), ROWS)
    for turn in range(1, ring):
        moves = [(i, (i + turn) % ring) for i in range(ring)]
        turns[turn] = lax.ppermute(turns[turn], "y", moves)
    heads = jax.ShapeDtypeStruct((seq_count, 3 * HD, tokens), jnp.bfloat16)
    heads_qkv = moved_call(place_kernel, "place", place, tuple(turns), heads).reshape(seq_count, 3, HD, tokens)
    own, heads_qkv, near = lax.optimization_barrier((own, heads_qkv, near))
    own = own.reshape(row_count * SHARE, width)
    other = lax.ppermute(own, "c", SWAP)
    grad_rows = project_call(core_id, own, other, dout, near, seq_count)
    grad_rows, heads_qkv = lax.optimization_barrier((grad_rows, heads_qkv))
    heads_grad = exchange(grad_rows, SEQ)
    probs = probs_call(heads_qkv)

    factor = float(tokens * seq_count * lax.axis_size(DP)) ** (-0.5)
    kept, sent = term_call(core_id, dout, attn_out, factor)
    sent = lax.ppermute(sent, "c", SWAP)
    pair = (kept.astype(jnp.float32) + sent.astype(jnp.float32)).astype(jnp.bfloat16)
    pair = pair.reshape(2, width // 2, pair.shape[1])
    sent = lax.ppermute(at(pair, 1 - side), "zl", SWAP)
    quad = (at(pair, side).astype(jnp.float32) + sent.astype(jnp.float32)).astype(jnp.bfloat16)
    quad, heads_grad, probs = lax.optimization_barrier((quad, heads_grad, probs))
    clip = exchange(quad.reshape(ring, cols, quad.shape[1]), "y")
    local = grads_call(heads_qkv, heads_grad, probs)
    local, clip = lax.optimization_barrier((local, clip))

    line, across = lax.axis_size("x"), lax.axis_size("zh")
    kind = jax.ShapeDtypeStruct((across, 24, LANES), jnp.float32)
    scratch = [pltpu.VMEM((line,) + kind.shape, jnp.float32)]
    pieces = moved_call(arrange_kernel, "arrange", place, (clip,), (kind,) * line, scratch)
    pieces = list(pieces)
    for turn in range(1, line):
        moves = [(i, (i + turn) % line) for i in range(line)]
        pieces[turn] = lax.ppermute(pieces[turn], "x", moves)
    block = jax.ShapeDtypeStruct(kind.shape[1:], jnp.float32)
    scratch = [pltpu.VMEM(kind.shape, jnp.float32)]
    pieces = moved_call(gather_kernel, "gather", place, tuple(pieces), (block,) * across, scratch)
    grad_new = jnp.zeros((24, LANES), jnp.float32)
    for turn in range(across):
        moves = [
            ((z * line + x) * 2 + c, (c * across + (z + turn) % across) * line + x)
            for z in range(across)
            for x in range(line)
            for c in range(2)
        ]
        grad_new = grad_new + lax.ppermute(pieces[turn], DP, moves)
    grad_new = grad_new[:rows, :cols]

    back = exchange(local, SEQ)
    dqkv = jnp.transpose(back, (3, 1, 0, 2)).reshape(tokens, 3, width)
    return (dqkv, grad_new, weight_new, moment_one, moment_two)


def solution(mesh):
    fine = Mesh(mesh.devices.reshape(4, 8, 2, 2, 8), ("zh", "x", "c", "zl", "y"))
    rows = P(DP + SEQ)
    square = P(DP, SEQ)
    return jax.shard_map(
        per_device,
        mesh=fine,
        in_specs=(rows, rows, rows, square, square, square, square),
        out_specs=(rows, square, square, square, square),
        check_vma=False,
    )
```

```python
import math

import jax
import jax.numpy as jnp
from jax import lax
from jax.experimental import pallas as pl
from jax.experimental.pallas import tpu as pltpu
from jax.sharding import Mesh, PartitionSpec as P

HD = 72
BLOCK = 256

BETA_ONE = 0.9
BETA_TWO = 0.999
LEARN_RATE = 0.001
ADAM_EPS = 1e-08
CORRECT_ONE = 0.999973438601112
CORRECT_TWO = 0.0952078528862904
LOG2_E = 1.4426950408889634


def probs_kernel(heads_ref, probs_ref, keys_ref):
    blocks = heads_ref.shape[0]
    width = heads_ref.shape[3]
    step = pl.program_id(0)

    @pl.when(step == 0)
    def _():
        for s in range(blocks):
            keys_ref[s * width : (s + 1) * width, :] = heads_ref[s, 1].T

    per = probs_ref.shape[1] // width
    queries = jnp.concatenate([heads_ref[step * per + j, 0] for j in range(per)], axis=1)
    scores = lax.dot_general(
        keys_ref[...], queries, (((1,), (0,)), ((), ())), preferred_element_type=jnp.float32
    )
    top = jnp.max(scores, axis=0, keepdims=True)
    weights = jnp.exp2((scores - top) * (HD ** (-0.5) * LOG2_E))
    total = jnp.sum(weights, axis=0, keepdims=True)
    probs_ref[...] = (weights * (1.0 / total)).astype(jnp.bfloat16)


def grads_kernel(
    heads_ref, grad_ref, probs_ref, out_ref, keys_ref, values_ref, grads_ref, dkeys_ref, dvalues_ref
):
    blocks = heads_ref.shape[0]
    width = heads_ref.shape[3]
    step = pl.program_id(0)
    per = probs_ref.shape[1] // width
    block = per * width
    factor = HD ** (-0.5)

    @pl.when(step == 0)
    def _():
        for s in range(blocks):
            keys_ref[:, s * width : (s + 1) * width] = heads_ref[s, 1]
            values_ref[s * width : (s + 1) * width, :] = heads_ref[s, 2].T
        dkeys_ref[...] = jnp.zeros_like(dkeys_ref)
        dvalues_ref[...] = jnp.zeros_like(dvalues_ref)
        count = HD // 2
        stride = grad_ref.shape[1] // 2
        dims = lax.broadcasted_iota(jnp.int32, (HD, stride), 0)
        order = lax.broadcasted_iota(jnp.int32, (HD, stride), 1)
        run = jnp.zeros_like(order)
        for k in range(1, count // SHARE):
            run += (order >= k * SHARE).astype(jnp.int32)
        side = blocks // 2
        parts = []
        for h in range(2):
            pieces = []
            for s in range(blocks):
                start = (h ^ (s // side)) * stride
                pieces.append(grad_ref[h * side + s % side, start : start + stride, :])
            choose = ((dims == order + SHARE * (run + h)) & (order < count)).astype(jnp.bfloat16)
            parts.append(
                lax.dot_general(
                    choose,
                    jnp.concatenate(pieces, axis=1),
                    (((1,), (0,)), ((), ())),
                    preferred_element_type=jnp.float32,
                )
            )
        placed = (parts[0] + parts[1]).astype(jnp.bfloat16)
        for b in range(pl.cdiv(blocks, per)):
            grads_ref[b] = placed[:, b * block : (b + 1) * block]

    grads_t = grads_ref[step]
    queries = jnp.concatenate([heads_ref[step * per + j, 0].T for j in range(per)], axis=0)
    half = probs_ref[...]
    grad_probs = lax.dot_general(
        values_ref[...], grads_t, (((1,), (0,)), ((), ())), preferred_element_type=jnp.float32
    )
    probs = half.astype(jnp.float32)
    row_dot = jnp.sum(probs * grad_probs, axis=0, keepdims=True)
    logits = (probs * (grad_probs - row_dot)).astype(jnp.bfloat16)
    dvalues_ref[...] += lax.dot_general(
        half, grads_t.T, (((1,), (0,)), ((), ())), preferred_element_type=jnp.float32
    )
    dkeys_ref[...] += lax.dot_general(
        logits, queries, (((1,), (0,)), ((), ())), preferred_element_type=jnp.float32
    )
    dqueries = factor * lax.dot_general(
        keys_ref[...], logits, (((1,), (0,)), ((), ())), preferred_element_type=jnp.float32
    )
    for j in range(per):
        out_ref[step * per + j, 0] = dqueries[:, j * width : (j + 1) * width].astype(jnp.bfloat16)

    @pl.when(step == pl.num_programs(0) - 1)
    def _():
        for s in range(blocks):
            out_ref[s, 1] = (dkeys_ref[s * width : (s + 1) * width, :].T * factor).astype(jnp.bfloat16)
            out_ref[s, 2] = dvalues_ref[s * width : (s + 1) * width, :].T.astype(jnp.bfloat16)


def whole(shape):
    return pl.BlockSpec(shape, lambda i: (0,) * len(shape))


def probs_call(heads):
    count, _, dims, width = heads.shape
    length = count * width
    block = min(BLOCK, length)
    return pl.pallas_call(
        probs_kernel,
        out_shape=jax.ShapeDtypeStruct((length, length), jnp.bfloat16),
        grid=(length // block,),
        in_specs=[whole(heads.shape)],
        out_specs=pl.BlockSpec((length, block), lambda i: (0, i)),
        scratch_shapes=[pltpu.VMEM((length, dims), jnp.bfloat16)],
        compiler_params=pltpu.CompilerParams(vmem_limit_bytes=48 * 2**20),
        cost_estimate=pl.CostEstimate(
            flops=2 * length * length * 256, transcendentals=length * length, bytes_accessed=2 * length * length
        ),
        name="probs",
    )(heads)


def grads_call(heads, grad, probs):
    count, _, dims, width = heads.shape
    length = count * width
    block = min(BLOCK, length)
    return pl.pallas_call(
        grads_kernel,
        out_shape=jax.ShapeDtypeStruct(heads.shape, jnp.bfloat16),
        grid=(length // block,),
        in_specs=[whole(heads.shape), whole(grad.shape), pl.BlockSpec((length, block), lambda i: (0, i))],
        out_specs=whole(heads.shape),
        scratch_shapes=[
            pltpu.VMEM((dims, length), jnp.bfloat16),
            pltpu.VMEM((length, dims), jnp.bfloat16),
            pltpu.VMEM((length // block, dims, block), jnp.bfloat16),
            pltpu.VMEM((length, dims), jnp.float32),
            pltpu.VMEM((length, dims), jnp.float32),
        ],
        compiler_params=pltpu.CompilerParams(vmem_limit_bytes=48 * 2**20),
        cost_estimate=pl.CostEstimate(
            flops=8 * length * length * 256, transcendentals=0, bytes_accessed=2 * length * length
        ),
        name="grads",
    )(heads, grad, probs)


def term_kernel(core_ref, dout_ref, out_in_ref, kept_ref, sent_ref, *, factor):
    half = out_in_ref.shape[1] // 2
    turned = dout_ref[...].T
    for side in range(2):
        product = lax.dot_general(
            turned,
            out_in_ref[:, side * half : (side + 1) * half],
            (((1,), (0,)), ((), ())),
            preferred_element_type=jnp.float32,
        )
        rounded = (product * factor).astype(jnp.bfloat16)
        if side == 0:
            kept_ref[:, half:] = jnp.zeros_like(kept_ref[:, half:])
            sent_ref[:, half:] = jnp.zeros_like(sent_ref[:, half:])

        @pl.when(core_ref[0] == side)
        def _():
            kept_ref[:, :half] = rounded

        @pl.when(core_ref[0] != side)
        def _():
            sent_ref[:, :half] = rounded


def term_call(core, dout, attn_out, factor):
    tokens, width = dout.shape
    kind = jax.ShapeDtypeStruct((width, pl.cdiv(width // 2, LANES) * LANES), jnp.bfloat16)
    vmem = pl.BlockSpec(memory_space=pltpu.VMEM)
    return pl.pallas_call(
        lambda *refs: term_kernel(*refs, factor=factor),
        out_shape=(kind, kind),
        in_specs=[pl.BlockSpec(memory_space=pltpu.SMEM), vmem, vmem],
        out_specs=(vmem, vmem),
        compiler_params=pltpu.CompilerParams(vmem_limit_bytes=32 * 2**20),
        cost_estimate=pl.CostEstimate(
            flops=2 * width * width * 256, transcendentals=0, bytes_accessed=2 * width * width
        ),
        name="term",
    )(core, dout, attn_out)


def project_kernel(core_ref, own_ref, other_ref, dout_ref, near_ref, out_ref, rows_ref):
    blocks = out_ref.shape[0] * 2
    width = dout_ref.shape[0]
    count = rows_ref.shape[2]
    tokens = jnp.concatenate([dout_ref[...], near_ref[...]], axis=0)
    for source, flip in ((own_ref, 0), (other_ref, 1)):
        product = lax.dot_general(
            source[...], tokens, (((1,), (1,)), ((), ())), preferred_element_type=jnp.float32
        )
        for parity in range(2):

            @pl.when(core_ref[0] == parity ^ flip)
            def _():
                for b in range(blocks):
                    start = ((b % 2) * 2 + parity) * SHARE
                    for side in range(2):
                        rows_ref[b // 2, side, start : start + SHARE, :] = product[
                            b * SHARE : (b + 1) * SHARE, side * width : (side + 1) * width
                        ]

    stride = out_ref.shape[1] // 2
    for side in range(2):
        out_ref[:, side * stride : side * stride + count, :] = rows_ref[:, side].astype(jnp.bfloat16)
        out_ref[:, side * stride + count : (side + 1) * stride, :] = jnp.zeros(
            (blocks // 2, stride - count, width), jnp.bfloat16
        )


def project_call(core, own, other, dout, near, heads):
    tokens, width = dout.shape
    count = 2 * own.shape[0] // heads
    shape = (heads, 2 * (pl.cdiv(count, 8) * 8), tokens)
    vmem = pl.BlockSpec(memory_space=pltpu.VMEM)
    return pl.pallas_call(
        project_kernel,
        out_shape=jax.ShapeDtypeStruct(shape, jnp.bfloat16),
        in_specs=[pl.BlockSpec(memory_space=pltpu.SMEM), vmem, vmem, vmem, vmem],
        out_specs=vmem,
        scratch_shapes=[pltpu.VMEM((heads, 2, count, tokens), jnp.float32)],
        compiler_params=pltpu.CompilerParams(vmem_limit_bytes=32 * 2**20),
        cost_estimate=pl.CostEstimate(
            flops=4 * width * width * tokens, transcendentals=0, bytes_accessed=4 * width * width
        ),
        name="project",
    )(core, own, other, dout, near)


def arrange_kernel(clip_ref, out_ref):
    line, across = out_ref.shape[0], out_ref.shape[1]
    cols = clip_ref.shape[1]
    total = clip_ref[0].astype(jnp.float32)
    for s in range(1, clip_ref.shape[0]):
        total = total + clip_ref[s].astype(jnp.float32)
    turned = total.T
    out_ref[...] = jnp.zeros_like(out_ref)
    for z in range(across):
        for x in range(line):
            start = (z * line + x) * ROWS_DEV
            out_ref[x, z, :ROWS_DEV, :cols] = turned[start : start + ROWS_DEV]


def arrange_call(clip, line, across):
    vmem = pl.BlockSpec(memory_space=pltpu.VMEM)
    return pl.pallas_call(
        arrange_kernel,
        out_shape=jax.ShapeDtypeStruct((line, across, 24, LANES), jnp.float32),
        in_specs=[vmem],
        out_specs=vmem,
        compiler_params=pltpu.CompilerParams(vmem_limit_bytes=16 * 2**20),
        cost_estimate=pl.CostEstimate(flops=0, transcendentals=0, bytes_accessed=0),
        name="arrange",
    )(clip)


SEQ = ("zl", "y")
ROWS = ("zh", "x")
DP = ("zh", "x", "c")
ROWS_DEV = 18
SHARE = 9
LANES = 128
SWAP = [(0, 1), (1, 0)]


def exchange(array, axes):
    return lax.all_to_all(array, axes, 0, 0, tiled=True)


def at(array, index):
    return lax.dynamic_index_in_dim(array, index, 0, keepdims=False)


def per_device(qkv, attn_out, dout, w_master, mom1, mom2, grad_prev):
    tokens, _, width = qkv.shape
    seq_count = lax.axis_size(SEQ)
    row_count = lax.axis_size(ROWS)
    ring = lax.axis_size("y")
    rows, cols = w_master.shape
    core, side = lax.axis_index("c"), lax.axis_index("zl")
    core_id = core[None].astype(jnp.int32)

    moment_one = BETA_ONE * mom1 + (1.0 - BETA_ONE) * grad_prev
    moment_two = BETA_TWO * mom2 + (1.0 - BETA_TWO) * grad_prev * grad_prev
    weight_new = w_master - LEARN_RATE * (moment_one / CORRECT_ONE) / (
        jnp.sqrt(moment_two / CORRECT_TWO) + ADAM_EPS
    )
    weight_half = weight_new.astype(jnp.bfloat16)

    by_head = jnp.transpose(qkv.reshape(tokens, 3, seq_count, HD), (2, 1, 3, 0)).reshape(seq_count, 3 * HD, tokens)
    size = SHARE * cols
    flat = jnp.pad(weight_half.reshape(2, size), ((0, 0), (0, 8 * LANES - size))).reshape(2, 1, 8, LANES)
    flat = jnp.broadcast_to(flat, (2, seq_count // 2, 8, LANES)).reshape(seq_count, 8, LANES)
    packed = jnp.concatenate([by_head, flat], axis=1)
    packed, dout, attn_out = lax.optimization_barrier((packed, dout, attn_out))
    arrived = exchange(packed, SEQ)
    heads_qkv = arrived[:, : 3 * HD].reshape(seq_count, 3, HD, tokens)
    columns = arrived[:, 3 * HD :].reshape(seq_count, 8 * LANES)[:, :size].reshape(seq_count, SHARE, cols)

    factor = float(tokens * seq_count * lax.axis_size(DP)) ** (-0.5)
    kept, sent = term_call(core_id, dout, attn_out, factor)
    sent = lax.ppermute(sent, "c", SWAP)
    pair = (kept.astype(jnp.float32) + sent.astype(jnp.float32)).astype(jnp.bfloat16)
    pair = pair.reshape(2, width // 2, pair.shape[1])
    sent = lax.ppermute(at(pair, 1 - side), "zl", SWAP)
    quad = (at(pair, side).astype(jnp.float32) + sent.astype(jnp.float32)).astype(jnp.bfloat16)

    lane = math.gcd(SHARE * width, LANES)
    row_block = jnp.transpose(columns, (1, 0, 2)).reshape(SHARE * width // lane, lane)
    near = lax.ppermute(dout, "zl", SWAP)
    row_block, quad, near = lax.optimization_barrier((row_block, quad, near))
    own = exchange(jnp.broadcast_to(row_block[None], (row_count,) + row_block.shape), ROWS)
    probs = probs_call(heads_qkv)
    own, probs, near = lax.optimization_barrier((own, probs, near))
    own = own.reshape(row_count * SHARE, width)
    other = lax.ppermute(own, "c", SWAP)
    grad_rows = project_call(core_id, own, other, dout, near, seq_count)
    heads_grad = exchange(grad_rows, SEQ)

    quad, heads_grad, probs = lax.optimization_barrier((quad, heads_grad, probs))
    clip = exchange(quad.reshape(ring, cols, quad.shape[1]), "y")
    local = grads_call(heads_qkv, heads_grad, probs)
    local, clip = lax.optimization_barrier((local, clip))

    line, across = lax.axis_size("x"), lax.axis_size("zh")
    pieces = arrange_call(clip, line, across)
    reach = line // 2
    while reach:
        bit = (lax.axis_index("x") // reach) % 2
        halves = pieces.reshape((2, reach) + pieces.shape[1:])
        sent = at(halves, 1 - bit).astype(jnp.bfloat16)
        sent = lax.ppermute(sent, "x", [(i, i ^ reach) for i in range(line)])
        pieces = at(halves, bit) + sent.astype(jnp.float32)
        reach //= 2
    pieces = pieces[0]
    grad_new = jnp.zeros((24, LANES), jnp.float32)
    for turn in range(across):
        moves = [
            ((z * line + x) * 2 + c, (c * across + (z + turn) % across) * line + x)
            for z in range(across)
            for x in range(line)
            for c in range(2)
        ]
        grad_new = grad_new + lax.ppermute(at(pieces, (lax.axis_index("zh") + turn) % across), DP, moves)
    grad_new = grad_new[:rows, :cols]

    back = exchange(local, SEQ)
    dqkv = jnp.transpose(back, (3, 1, 0, 2)).reshape(tokens, 3, width)
    return (dqkv, grad_new, weight_new, moment_one, moment_two)


def solution(mesh):
    fine = Mesh(mesh.devices.reshape(4, 8, 2, 2, 8), ("zh", "x", "c", "zl", "y"))
    rows = P(DP + SEQ)
    square = P(DP, SEQ)
    return jax.shard_map(
        per_device,
        mesh=fine,
        in_specs=(rows, rows, rows, square, square, square, square),
        out_specs=(rows, square, square, square, square),
        check_vma=False,
    )
```

```python
import math

import jax
import jax.numpy as jnp
from jax import lax
from jax.experimental import pallas as pl
from jax.experimental.pallas import tpu as pltpu
from jax.sharding import Mesh, PartitionSpec as P

HD = 72
BLOCK = 256

BETA_ONE = 0.9
BETA_TWO = 0.999
LEARN_RATE = 0.001
ADAM_EPS = 1e-08
CORRECT_ONE = 0.999973438601112
CORRECT_TWO = 0.0952078528862904
LOG2_E = 1.4426950408889634


def probs_kernel(heads_ref, probs_ref, keys_ref):
    blocks = heads_ref.shape[0]
    width = heads_ref.shape[3]
    step = pl.program_id(0)

    @pl.when(step == 0)
    def _():
        for s in range(blocks):
            keys_ref[s * width : (s + 1) * width, :] = heads_ref[s, 1].T

    per = probs_ref.shape[1] // width
    queries = jnp.concatenate([heads_ref[step * per + j, 0] for j in range(per)], axis=1)
    scores = lax.dot_general(
        keys_ref[...], queries, (((1,), (0,)), ((), ())), preferred_element_type=jnp.float32
    )
    top = jnp.max(scores, axis=0, keepdims=True)
    weights = jnp.exp2((scores - top) * (HD ** (-0.5) * LOG2_E))
    total = jnp.sum(weights, axis=0, keepdims=True)
    probs_ref[...] = (weights * (1.0 / total)).astype(jnp.bfloat16)


def grads_kernel(
    heads_ref, grad_ref, probs_ref, out_ref, keys_ref, values_ref, grads_ref, dkeys_ref, dvalues_ref
):
    blocks = heads_ref.shape[0]
    width = heads_ref.shape[3]
    step = pl.program_id(0)
    per = probs_ref.shape[1] // width
    block = per * width
    factor = HD ** (-0.5)

    @pl.when(step == 0)
    def _():
        for s in range(blocks):
            keys_ref[:, s * width : (s + 1) * width] = heads_ref[s, 1]
            values_ref[s * width : (s + 1) * width, :] = heads_ref[s, 2].T
        dkeys_ref[...] = jnp.zeros_like(dkeys_ref)
        dvalues_ref[...] = jnp.zeros_like(dvalues_ref)
        count = HD // 2
        stride = grad_ref.shape[1] // 2
        dims = lax.broadcasted_iota(jnp.int32, (HD, stride), 0)
        order = lax.broadcasted_iota(jnp.int32, (HD, stride), 1)
        run = jnp.zeros_like(order)
        for k in range(1, count // SHARE):
            run += (order >= k * SHARE).astype(jnp.int32)
        side = blocks // 2
        parts = []
        for h in range(2):
            pieces = []
            for s in range(blocks):
                start = (h ^ (s // side)) * stride
                pieces.append(grad_ref[h * side + s % side, start : start + stride, :])
            choose = ((dims == order + SHARE * (run + h)) & (order < count)).astype(jnp.bfloat16)
            parts.append(
                lax.dot_general(
                    choose,
                    jnp.concatenate(pieces, axis=1),
                    (((1,), (0,)), ((), ())),
                    preferred_element_type=jnp.float32,
                )
            )
        placed = (parts[0] + parts[1]).astype(jnp.bfloat16)
        for b in range(pl.cdiv(blocks, per)):
            grads_ref[b] = placed[:, b * block : (b + 1) * block]

    grads_t = grads_ref[step]
    queries = jnp.concatenate([heads_ref[step * per + j, 0].T for j in range(per)], axis=0)
    half = probs_ref[...]
    grad_probs = lax.dot_general(
        values_ref[...], grads_t, (((1,), (0,)), ((), ())), preferred_element_type=jnp.float32
    )
    probs = half.astype(jnp.float32)
    row_dot = jnp.sum(probs * grad_probs, axis=0, keepdims=True)
    logits = (probs * (grad_probs - row_dot)).astype(jnp.bfloat16)
    dvalues_ref[...] += lax.dot_general(
        half, grads_t.T, (((1,), (0,)), ((), ())), preferred_element_type=jnp.float32
    )
    dkeys_ref[...] += lax.dot_general(
        logits, queries, (((1,), (0,)), ((), ())), preferred_element_type=jnp.float32
    )
    dqueries = factor * lax.dot_general(
        keys_ref[...], logits, (((1,), (0,)), ((), ())), preferred_element_type=jnp.float32
    )
    for j in range(per):
        out_ref[step * per + j, 0] = dqueries[:, j * width : (j + 1) * width].astype(jnp.bfloat16)

    @pl.when(step == pl.num_programs(0) - 1)
    def _():
        for s in range(blocks):
            out_ref[s, 1] = (dkeys_ref[s * width : (s + 1) * width, :].T * factor).astype(jnp.bfloat16)
            out_ref[s, 2] = dvalues_ref[s * width : (s + 1) * width, :].T.astype(jnp.bfloat16)


def whole(shape):
    return pl.BlockSpec(shape, lambda i: (0,) * len(shape))


def probs_call(heads):
    count, _, dims, width = heads.shape
    length = count * width
    block = min(BLOCK, length)
    return pl.pallas_call(
        probs_kernel,
        out_shape=jax.ShapeDtypeStruct((length, length), jnp.bfloat16),
        grid=(length // block,),
        in_specs=[whole(heads.shape)],
        out_specs=pl.BlockSpec((length, block), lambda i: (0, i)),
        scratch_shapes=[pltpu.VMEM((length, dims), jnp.bfloat16)],
        compiler_params=pltpu.CompilerParams(vmem_limit_bytes=48 * 2**20),
        cost_estimate=pl.CostEstimate(
            flops=2 * length * length * 256, transcendentals=length * length, bytes_accessed=2 * length * length
        ),
        name="probs",
    )(heads)


def grads_call(heads, grad, probs):
    count, _, dims, width = heads.shape
    length = count * width
    block = min(BLOCK, length)
    return pl.pallas_call(
        grads_kernel,
        out_shape=jax.ShapeDtypeStruct(heads.shape, jnp.bfloat16),
        grid=(length // block,),
        in_specs=[whole(heads.shape), whole(grad.shape), pl.BlockSpec((length, block), lambda i: (0, i))],
        out_specs=whole(heads.shape),
        scratch_shapes=[
            pltpu.VMEM((dims, length), jnp.bfloat16),
            pltpu.VMEM((length, dims), jnp.bfloat16),
            pltpu.VMEM((length // block, dims, block), jnp.bfloat16),
            pltpu.VMEM((length, dims), jnp.float32),
            pltpu.VMEM((length, dims), jnp.float32),
        ],
        compiler_params=pltpu.CompilerParams(vmem_limit_bytes=48 * 2**20),
        cost_estimate=pl.CostEstimate(
            flops=8 * length * length * 256, transcendentals=0, bytes_accessed=2 * length * length
        ),
        name="grads",
    )(heads, grad, probs)


def term_kernel(core_ref, dout_ref, out_in_ref, kept_ref, sent_ref, *, factor):
    half = out_in_ref.shape[1] // 2
    turned = dout_ref[...].T
    for side in range(2):
        product = lax.dot_general(
            turned,
            out_in_ref[:, side * half : (side + 1) * half],
            (((1,), (0,)), ((), ())),
            preferred_element_type=jnp.float32,
        )
        rounded = (product * factor).astype(jnp.bfloat16)
        if side == 0:
            kept_ref[:, half:] = jnp.zeros_like(kept_ref[:, half:])
            sent_ref[:, half:] = jnp.zeros_like(sent_ref[:, half:])

        @pl.when(core_ref[0] == side)
        def _():
            kept_ref[:, :half] = rounded

        @pl.when(core_ref[0] != side)
        def _():
            sent_ref[:, :half] = rounded


def term_call(core, dout, attn_out, factor):
    tokens, width = dout.shape
    kind = jax.ShapeDtypeStruct((width, pl.cdiv(width // 2, LANES) * LANES), jnp.bfloat16)
    vmem = pl.BlockSpec(memory_space=pltpu.VMEM)
    return pl.pallas_call(
        lambda *refs: term_kernel(*refs, factor=factor),
        out_shape=(kind, kind),
        in_specs=[pl.BlockSpec(memory_space=pltpu.SMEM), vmem, vmem],
        out_specs=(vmem, vmem),
        compiler_params=pltpu.CompilerParams(vmem_limit_bytes=32 * 2**20),
        cost_estimate=pl.CostEstimate(
            flops=2 * width * width * 256, transcendentals=0, bytes_accessed=2 * width * width
        ),
        name="term",
    )(core, dout, attn_out)


def project_kernel(core_ref, own_ref, other_ref, dout_ref, near_ref, out_ref, rows_ref):
    blocks = out_ref.shape[0] * 2
    width = dout_ref.shape[0]
    count = rows_ref.shape[2]
    tokens = jnp.concatenate([dout_ref[...], near_ref[...]], axis=0)
    for source, flip in ((own_ref, 0), (other_ref, 1)):
        product = lax.dot_general(
            source[...], tokens, (((1,), (1,)), ((), ())), preferred_element_type=jnp.float32
        )
        for parity in range(2):

            @pl.when(core_ref[0] == parity ^ flip)
            def _():
                for b in range(blocks):
                    start = ((b % 2) * 2 + parity) * SHARE
                    for side in range(2):
                        rows_ref[b // 2, side, start : start + SHARE, :] = product[
                            b * SHARE : (b + 1) * SHARE, side * width : (side + 1) * width
                        ]

    stride = out_ref.shape[1] // 2
    for side in range(2):
        out_ref[:, side * stride : side * stride + count, :] = rows_ref[:, side].astype(jnp.bfloat16)
        out_ref[:, side * stride + count : (side + 1) * stride, :] = jnp.zeros(
            (blocks // 2, stride - count, width), jnp.bfloat16
        )


def project_call(core, own, other, dout, near, heads):
    tokens, width = dout.shape
    count = 2 * own.shape[0] // heads
    shape = (heads, 2 * (pl.cdiv(count, 8) * 8), tokens)
    vmem = pl.BlockSpec(memory_space=pltpu.VMEM)
    return pl.pallas_call(
        project_kernel,
        out_shape=jax.ShapeDtypeStruct(shape, jnp.bfloat16),
        in_specs=[pl.BlockSpec(memory_space=pltpu.SMEM), vmem, vmem, vmem, vmem],
        out_specs=vmem,
        scratch_shapes=[pltpu.VMEM((heads, 2, count, tokens), jnp.float32)],
        compiler_params=pltpu.CompilerParams(vmem_limit_bytes=32 * 2**20),
        cost_estimate=pl.CostEstimate(
            flops=4 * width * width * tokens, transcendentals=0, bytes_accessed=4 * width * width
        ),
        name="project",
    )(core, own, other, dout, near)


def arrange_kernel(clip_ref, out_ref, blocks_ref):
    line, across, high = blocks_ref.shape[0], blocks_ref.shape[1], blocks_ref.shape[2]
    cols = clip_ref.shape[1]
    turned = clip_ref[0].T
    blocks_ref[...] = jnp.zeros_like(blocks_ref)
    for z in range(across):
        for x in range(line):
            start = (z * line + x) * ROWS_DEV
            blocks_ref[x, z, :ROWS_DEV, :cols] = turned[start : start + ROWS_DEV]
    for z in range(across):
        out_ref[:, z * high : (z + 1) * high, :] = blocks_ref[:, z].astype(jnp.bfloat16)


def arrange_call(clip, line, across):
    vmem = pl.BlockSpec(memory_space=pltpu.VMEM)
    return pl.pallas_call(
        arrange_kernel,
        out_shape=jax.ShapeDtypeStruct((line, across * 24, LANES), jnp.bfloat16),
        in_specs=[vmem],
        out_specs=vmem,
        scratch_shapes=[pltpu.VMEM((line, across, 24, LANES), jnp.float32)],
        compiler_params=pltpu.CompilerParams(vmem_limit_bytes=16 * 2**20),
        cost_estimate=pl.CostEstimate(flops=0, transcendentals=0, bytes_accessed=0),
        name="arrange",
    )(clip)


def halve(pieces, axis, turn):
    bit = (lax.axis_index(axis) >> turn) % 2
    pairs = pieces.reshape((pieces.shape[0] // 2, 2) + pieces.shape[1:])
    moves = [(i, i ^ (1 << turn)) for i in range(lax.axis_size(axis))]
    sent = lax.dynamic_index_in_dim(pairs, 1 - bit, 1, keepdims=False).astype(jnp.bfloat16)
    kept = lax.dynamic_index_in_dim(pairs, bit, 1, keepdims=False)
    return kept.astype(jnp.float32) + lax.ppermute(sent, axis, moves).astype(jnp.float32)


SEQ = ("zl", "y")
ROWS = ("zh", "x")
DP = ("zh", "x", "c")
ROWS_DEV = 18
SHARE = 9
LANES = 128
SWAP = [(0, 1), (1, 0)]


def exchange(array, axes):
    return lax.all_to_all(array, axes, 0, 0, tiled=True)


def at(array, index):
    return lax.dynamic_index_in_dim(array, index, 0, keepdims=False)


def per_device(qkv, attn_out, dout, w_master, mom1, mom2, grad_prev):
    tokens, _, width = qkv.shape
    seq_count = lax.axis_size(SEQ)
    row_count = lax.axis_size(ROWS)
    ring = lax.axis_size("y")
    rows, cols = w_master.shape
    core, side = lax.axis_index("c"), lax.axis_index("zl")
    core_id = core[None].astype(jnp.int32)

    moment_one = BETA_ONE * mom1 + (1.0 - BETA_ONE) * grad_prev
    moment_two = BETA_TWO * mom2 + (1.0 - BETA_TWO) * grad_prev * grad_prev
    weight_new = w_master - LEARN_RATE * (moment_one / CORRECT_ONE) / (
        jnp.sqrt(moment_two / CORRECT_TWO) + ADAM_EPS
    )
    weight_half = weight_new.astype(jnp.bfloat16)

    by_head = jnp.transpose(qkv.reshape(tokens, 3, seq_count, HD), (2, 1, 3, 0)).reshape(seq_count, 3 * HD, tokens)
    size = SHARE * cols
    flat = jnp.pad(weight_half.reshape(2, size), ((0, 0), (0, 8 * LANES - size))).reshape(2, 1, 8, LANES)
    flat = jnp.broadcast_to(flat, (2, seq_count // 2, 8, LANES)).reshape(seq_count, 8, LANES)
    packed = jnp.concatenate([by_head, flat], axis=1)
    packed, dout, attn_out = lax.optimization_barrier((packed, dout, attn_out))
    arrived = exchange(packed, SEQ)
    heads_qkv = arrived[:, : 3 * HD].reshape(seq_count, 3, HD, tokens)
    columns = arrived[:, 3 * HD :].reshape(seq_count, 8 * LANES)[:, :size].reshape(seq_count, SHARE, cols)

    factor = float(tokens * seq_count * lax.axis_size(DP)) ** (-0.5)
    kept, sent = term_call(core_id, dout, attn_out, factor)
    sent = lax.ppermute(sent, "c", SWAP)
    pair = (kept.astype(jnp.float32) + sent.astype(jnp.float32)).astype(jnp.bfloat16)
    pair = pair.reshape(2, width // 2, pair.shape[1])
    sent = lax.ppermute(at(pair, 1 - side), "zl", SWAP)
    quad = (at(pair, side).astype(jnp.float32) + sent.astype(jnp.float32)).astype(jnp.bfloat16)

    lane = math.gcd(SHARE * width, LANES)
    row_block = jnp.transpose(columns, (1, 0, 2)).reshape(SHARE * width // lane, lane)
    near = lax.ppermute(dout, "zl", SWAP)
    row_block, quad = lax.optimization_barrier((row_block, quad))
    own = exchange(jnp.broadcast_to(row_block[None], (row_count,) + row_block.shape), ROWS)
    probs = probs_call(heads_qkv)
    clip = halve(quad.reshape(ring, cols, quad.shape[1]), "y", 0)
    own, probs, near, clip = lax.optimization_barrier((own, probs, near, clip))
    own = own.reshape(row_count * SHARE, width)
    other = lax.ppermute(own, "c", SWAP)
    grad_rows = project_call(core_id, own, other, dout, near, seq_count)
    heads_grad = exchange(grad_rows, SEQ)

    line, across = lax.axis_size("x"), lax.axis_size("zh")
    clip, _ = lax.optimization_barrier((clip, grad_rows))
    step = lax.axis_index("y") // 2
    total = at(clip, step)
    for turn in range(1, ring // 2):
        moves = [(i, (i + 2 * turn) % ring) for i in range(ring)]
        sent = lax.ppermute(at(clip, (step + turn) % (ring // 2)).astype(jnp.bfloat16), "y", moves)
        total = total + sent.astype(jnp.float32)
    pieces = arrange_call(total[None], line, across)
    pieces, heads_grad, probs = lax.optimization_barrier((pieces, heads_grad, probs))
    pieces = exchange(pieces, "x")
    local = grads_call(heads_qkv, heads_grad, probs)
    local, pieces = lax.optimization_barrier((local, pieces))

    pieces = jnp.sum(pieces.astype(jnp.float32), axis=0).reshape(across, 24, LANES)
    grad_new = jnp.zeros((24, LANES), jnp.float32)
    for turn in range(across):
        moves = [
            ((z * line + x) * 2 + c, (c * across + (z + turn) % across) * line + x)
            for z in range(across)
            for x in range(line)
            for c in range(2)
        ]
        grad_new = grad_new + lax.ppermute(at(pieces, (lax.axis_index("zh") + turn) % across), DP, moves)
    grad_new = grad_new[:rows, :cols]

    back = exchange(local, SEQ)
    dqkv = jnp.transpose(back, (3, 1, 0, 2)).reshape(tokens, 3, width)
    return (dqkv, grad_new, weight_new, moment_one, moment_two)


def solution(mesh):
    fine = Mesh(mesh.devices.reshape(4, 8, 2, 2, 8), ("zh", "x", "c", "zl", "y"))
    rows = P(DP + SEQ)
    square = P(DP, SEQ)
    return jax.shard_map(
        per_device,
        mesh=fine,
        in_specs=(rows, rows, rows, square, square, square, square),
        out_specs=(rows, square, square, square, square),
        check_vma=False,
    )
```

```python
import math

import jax
import jax.numpy as jnp
from jax import lax
from jax.experimental import pallas as pl
from jax.experimental.pallas import tpu as pltpu
from jax.sharding import Mesh, PartitionSpec as P

HD = 72
BLOCK = 512

BETA_ONE = 0.9
BETA_TWO = 0.999
LEARN_RATE = 0.001
ADAM_EPS = 1e-08
CORRECT_ONE = 0.999973438601112
CORRECT_TWO = 0.0952078528862904
LOG2_E = 1.4426950408889634


def probs_kernel(heads_ref, probs_ref, keys_ref):
    blocks = heads_ref.shape[0]
    width = heads_ref.shape[3]
    step = pl.program_id(0)

    @pl.when(step == 0)
    def _():
        for s in range(blocks):
            keys_ref[s * width : (s + 1) * width, :] = heads_ref[s, 1].T

    per = probs_ref.shape[1] // width
    queries = jnp.concatenate([heads_ref[step * per + j, 0] for j in range(per)], axis=1)
    scores = lax.dot_general(
        keys_ref[...], queries, (((1,), (0,)), ((), ())), preferred_element_type=jnp.float32
    )
    top = jnp.max(scores, axis=0, keepdims=True)
    weights = jnp.exp2((scores - top) * (HD ** (-0.5) * LOG2_E))
    total = jnp.sum(weights, axis=0, keepdims=True)
    probs_ref[...] = (weights * (1.0 / total)).astype(jnp.bfloat16)


def grads_kernel(
    heads_ref, grad_ref, probs_ref, out_ref, keys_ref, values_ref, grads_ref, dkeys_ref, dvalues_ref
):
    blocks = heads_ref.shape[0]
    width = heads_ref.shape[3]
    step = pl.program_id(0)
    per = probs_ref.shape[1] // width
    block = per * width
    factor = HD ** (-0.5)

    @pl.when(step == 0)
    def _():
        for s in range(blocks):
            keys_ref[:, s * width : (s + 1) * width] = heads_ref[s, 1]
            values_ref[s * width : (s + 1) * width, :] = heads_ref[s, 2].T
        dkeys_ref[...] = jnp.zeros_like(dkeys_ref)
        dvalues_ref[...] = jnp.zeros_like(dvalues_ref)
        count = HD // 2
        stride = grad_ref.shape[1] // 2
        dims = lax.broadcasted_iota(jnp.int32, (HD, stride), 0)
        order = lax.broadcasted_iota(jnp.int32, (HD, stride), 1)
        run = jnp.zeros_like(order)
        for k in range(1, count // SHARE):
            run += (order >= k * SHARE).astype(jnp.int32)
        side = blocks // 2
        parts = []
        for h in range(2):
            pieces = []
            for s in range(blocks):
                start = (h ^ (s // side)) * stride
                pieces.append(grad_ref[h * side + s % side, start : start + stride, :])
            choose = ((dims == order + SHARE * (run + h)) & (order < count)).astype(jnp.bfloat16)
            parts.append(
                lax.dot_general(
                    choose,
                    jnp.concatenate(pieces, axis=1),
                    (((1,), (0,)), ((), ())),
                    preferred_element_type=jnp.float32,
                )
            )
        placed = (parts[0] + parts[1]).astype(jnp.bfloat16)
        for b in range(pl.cdiv(blocks, per)):
            grads_ref[b] = placed[:, b * block : (b + 1) * block]

    grads_t = grads_ref[step]
    queries = jnp.concatenate([heads_ref[step * per + j, 0].T for j in range(per)], axis=0)
    half = probs_ref[...]
    grad_probs = lax.dot_general(
        values_ref[...], grads_t, (((1,), (0,)), ((), ())), preferred_element_type=jnp.float32
    )
    probs = half.astype(jnp.float32)
    row_dot = jnp.sum(probs * grad_probs, axis=0, keepdims=True)
    logits = (probs * (grad_probs - row_dot)).astype(jnp.bfloat16)
    dvalues_ref[...] += lax.dot_general(
        half, grads_t.T, (((1,), (0,)), ((), ())), preferred_element_type=jnp.float32
    )
    dkeys_ref[...] += lax.dot_general(
        logits, queries, (((1,), (0,)), ((), ())), preferred_element_type=jnp.float32
    )
    dqueries = factor * lax.dot_general(
        keys_ref[...], logits, (((1,), (0,)), ((), ())), preferred_element_type=jnp.float32
    )
    for j in range(per):
        out_ref[step * per + j, 0] = dqueries[:, j * width : (j + 1) * width].astype(jnp.bfloat16)

    @pl.when(step == pl.num_programs(0) - 1)
    def _():
        for s in range(blocks):
            out_ref[s, 1] = (dkeys_ref[s * width : (s + 1) * width, :].T * factor).astype(jnp.bfloat16)
            out_ref[s, 2] = dvalues_ref[s * width : (s + 1) * width, :].T.astype(jnp.bfloat16)


def whole(shape):
    return pl.BlockSpec(shape, lambda i: (0,) * len(shape))


def probs_call(heads):
    count, _, dims, width = heads.shape
    length = count * width
    block = min(BLOCK, length)
    return pl.pallas_call(
        probs_kernel,
        out_shape=jax.ShapeDtypeStruct((length, length), jnp.bfloat16),
        grid=(length // block,),
        in_specs=[whole(heads.shape)],
        out_specs=pl.BlockSpec((length, block), lambda i: (0, i)),
        scratch_shapes=[pltpu.VMEM((length, dims), jnp.bfloat16)],
        compiler_params=pltpu.CompilerParams(vmem_limit_bytes=48 * 2**20),
        cost_estimate=pl.CostEstimate(
            flops=2 * length * length * 256, transcendentals=length * length, bytes_accessed=2 * length * length
        ),
        name="probs",
    )(heads)


def grads_call(heads, grad, probs):
    count, _, dims, width = heads.shape
    length = count * width
    block = min(BLOCK, length)
    return pl.pallas_call(
        grads_kernel,
        out_shape=jax.ShapeDtypeStruct(heads.shape, jnp.bfloat16),
        grid=(length // block,),
        in_specs=[whole(heads.shape), whole(grad.shape), pl.BlockSpec((length, block), lambda i: (0, i))],
        out_specs=whole(heads.shape),
        scratch_shapes=[
            pltpu.VMEM((dims, length), jnp.bfloat16),
            pltpu.VMEM((length, dims), jnp.bfloat16),
            pltpu.VMEM((length // block, dims, block), jnp.bfloat16),
            pltpu.VMEM((length, dims), jnp.float32),
            pltpu.VMEM((length, dims), jnp.float32),
        ],
        compiler_params=pltpu.CompilerParams(vmem_limit_bytes=48 * 2**20),
        cost_estimate=pl.CostEstimate(
            flops=8 * length * length * 256, transcendentals=0, bytes_accessed=2 * length * length
        ),
        name="grads",
    )(heads, grad, probs)


def term_kernel(core_ref, dout_ref, out_in_ref, kept_ref, sent_ref, *, factor):
    half = out_in_ref.shape[1] // 2
    turned = dout_ref[...].T
    for side in range(2):
        product = lax.dot_general(
            turned,
            out_in_ref[:, side * half : (side + 1) * half],
            (((1,), (0,)), ((), ())),
            preferred_element_type=jnp.float32,
        )
        rounded = (product * factor).astype(jnp.bfloat16)
        if side == 0:
            kept_ref[:, half:] = jnp.zeros_like(kept_ref[:, half:])
            sent_ref[:, half:] = jnp.zeros_like(sent_ref[:, half:])

        @pl.when(core_ref[0] == side)
        def _():
            kept_ref[:, :half] = rounded

        @pl.when(core_ref[0] != side)
        def _():
            sent_ref[:, :half] = rounded


def term_call(core, dout, attn_out, factor):
    tokens, width = dout.shape
    kind = jax.ShapeDtypeStruct((width, pl.cdiv(width // 2, LANES) * LANES), jnp.bfloat16)
    vmem = pl.BlockSpec(memory_space=pltpu.VMEM)
    return pl.pallas_call(
        lambda *refs: term_kernel(*refs, factor=factor),
        out_shape=(kind, kind),
        in_specs=[pl.BlockSpec(memory_space=pltpu.SMEM), vmem, vmem],
        out_specs=(vmem, vmem),
        compiler_params=pltpu.CompilerParams(vmem_limit_bytes=32 * 2**20),
        cost_estimate=pl.CostEstimate(
            flops=2 * width * width * 256, transcendentals=0, bytes_accessed=2 * width * width
        ),
        name="term",
    )(core, dout, attn_out)


def project_kernel(core_ref, own_ref, other_ref, dout_ref, near_ref, out_ref, rows_ref):
    blocks = out_ref.shape[0] * 2
    width = dout_ref.shape[0]
    count = rows_ref.shape[2]
    tokens = jnp.concatenate([dout_ref[...], near_ref[...]], axis=0)
    for source, flip in ((own_ref, 0), (other_ref, 1)):
        product = lax.dot_general(
            source[...], tokens, (((1,), (1,)), ((), ())), preferred_element_type=jnp.float32
        )
        for parity in range(2):

            @pl.when(core_ref[0] == parity ^ flip)
            def _():
                for b in range(blocks):
                    start = ((b % 2) * 2 + parity) * SHARE
                    for side in range(2):
                        rows_ref[b // 2, side, start : start + SHARE, :] = product[
                            b * SHARE : (b + 1) * SHARE, side * width : (side + 1) * width
                        ]

    stride = out_ref.shape[1] // 2
    for side in range(2):
        out_ref[:, side * stride : side * stride + count, :] = rows_ref[:, side].astype(jnp.bfloat16)
        out_ref[:, side * stride + count : (side + 1) * stride, :] = jnp.zeros(
            (blocks // 2, stride - count, width), jnp.bfloat16
        )


def project_call(core, own, other, dout, near, heads):
    tokens, width = dout.shape
    count = 2 * own.shape[0] // heads
    shape = (heads, 2 * (pl.cdiv(count, 8) * 8), tokens)
    vmem = pl.BlockSpec(memory_space=pltpu.VMEM)
    return pl.pallas_call(
        project_kernel,
        out_shape=jax.ShapeDtypeStruct(shape, jnp.bfloat16),
        in_specs=[pl.BlockSpec(memory_space=pltpu.SMEM), vmem, vmem, vmem, vmem],
        out_specs=vmem,
        scratch_shapes=[pltpu.VMEM((heads, 2, count, tokens), jnp.float32)],
        compiler_params=pltpu.CompilerParams(vmem_limit_bytes=32 * 2**20),
        cost_estimate=pl.CostEstimate(
            flops=4 * width * width * tokens, transcendentals=0, bytes_accessed=4 * width * width
        ),
        name="project",
    )(core, own, other, dout, near)


def arrange_kernel(clip_ref, out_ref, blocks_ref):
    line, across, high = blocks_ref.shape[0], blocks_ref.shape[1], blocks_ref.shape[2]
    cols = clip_ref.shape[1]
    total = clip_ref[0].astype(jnp.float32)
    for s in range(1, clip_ref.shape[0]):
        total = total + clip_ref[s].astype(jnp.float32)
    turned = total.T
    blocks_ref[...] = jnp.zeros_like(blocks_ref)
    for z in range(across):
        for x in range(line):
            start = (z * line + x) * ROWS_DEV
            blocks_ref[x, z, :ROWS_DEV, :cols] = turned[start : start + ROWS_DEV]
    for z in range(across):
        out_ref[:, z * high : (z + 1) * high, :] = blocks_ref[:, z].astype(jnp.bfloat16)


def arrange_call(clip, line, across):
    vmem = pl.BlockSpec(memory_space=pltpu.VMEM)
    return pl.pallas_call(
        arrange_kernel,
        out_shape=jax.ShapeDtypeStruct((line, across * 24, LANES), jnp.bfloat16),
        in_specs=[vmem],
        out_specs=vmem,
        scratch_shapes=[pltpu.VMEM((line, across, 24, LANES), jnp.float32)],
        compiler_params=pltpu.CompilerParams(vmem_limit_bytes=16 * 2**20),
        cost_estimate=pl.CostEstimate(flops=0, transcendentals=0, bytes_accessed=0),
        name="arrange",
    )(clip)


def halve(pieces, axis, turn):
    bit = (lax.axis_index(axis) >> turn) % 2
    pairs = pieces.reshape((pieces.shape[0] // 2, 2) + pieces.shape[1:])
    moves = [(i, i ^ (1 << turn)) for i in range(lax.axis_size(axis))]
    sent = lax.dynamic_index_in_dim(pairs, 1 - bit, 1, keepdims=False).astype(jnp.bfloat16)
    kept = lax.dynamic_index_in_dim(pairs, bit, 1, keepdims=False)
    return kept.astype(jnp.float32) + lax.ppermute(sent, axis, moves).astype(jnp.float32)


SEQ = ("zl", "yh", "yl")
ROWS = ("zh", "x")
DP = ("zh", "x", "c")
ROWS_DEV = 18
SHARE = 9
LANES = 128
SWAP = [(0, 1), (1, 0)]


def exchange(array, axes):
    return lax.all_to_all(array, axes, 0, 0, tiled=True)


def at(array, index):
    return lax.dynamic_index_in_dim(array, index, 0, keepdims=False)


def per_device(qkv, attn_out, dout, w_master, mom1, mom2, grad_prev):
    tokens, _, width = qkv.shape
    seq_count = lax.axis_size(SEQ)
    row_count = lax.axis_size(ROWS)
    ring = lax.axis_size(("yh", "yl"))
    rows, cols = w_master.shape
    core, side = lax.axis_index("c"), lax.axis_index("zl")
    core_id = core[None].astype(jnp.int32)

    moment_one = BETA_ONE * mom1 + (1.0 - BETA_ONE) * grad_prev
    moment_two = BETA_TWO * mom2 + (1.0 - BETA_TWO) * grad_prev * grad_prev
    weight_new = w_master - LEARN_RATE * (moment_one / CORRECT_ONE) / (
        jnp.sqrt(moment_two / CORRECT_TWO) + ADAM_EPS
    )
    weight_half = weight_new.astype(jnp.bfloat16)

    by_head = jnp.transpose(qkv.reshape(tokens, 3, seq_count, HD), (2, 1, 3, 0)).reshape(seq_count, 3 * HD, tokens)
    size = SHARE * cols
    flat = jnp.pad(weight_half.reshape(2, size), ((0, 0), (0, 8 * LANES - size))).reshape(2, 1, 8, LANES)
    flat = jnp.broadcast_to(flat, (2, seq_count // 2, 8, LANES)).reshape(seq_count, 8, LANES)
    packed = jnp.concatenate([by_head, flat], axis=1)
    packed, dout, attn_out = lax.optimization_barrier((packed, dout, attn_out))
    arrived = exchange(packed, SEQ)
    heads_qkv = arrived[:, : 3 * HD].reshape(seq_count, 3, HD, tokens)
    columns = arrived[:, 3 * HD :].reshape(seq_count, 8 * LANES)[:, :size].reshape(seq_count, SHARE, cols)

    factor = float(tokens * seq_count * lax.axis_size(DP)) ** (-0.5)
    kept, sent = term_call(core_id, dout, attn_out, factor)
    sent = lax.ppermute(sent, "c", SWAP)
    pair = (kept.astype(jnp.float32) + sent.astype(jnp.float32)).astype(jnp.bfloat16)
    pair = pair.reshape(2, width // 2, pair.shape[1])
    sent = lax.ppermute(at(pair, 1 - side), "zl", SWAP)
    quad = (at(pair, side).astype(jnp.float32) + sent.astype(jnp.float32)).astype(jnp.bfloat16)

    lane = math.gcd(SHARE * width, LANES)
    row_block = jnp.transpose(columns, (1, 0, 2)).reshape(SHARE * width // lane, lane)
    near = lax.ppermute(dout, "zl", SWAP)
    row_block, quad = lax.optimization_barrier((row_block, quad))
    own = exchange(jnp.broadcast_to(row_block[None], (row_count,) + row_block.shape), ROWS)
    probs = probs_call(heads_qkv)
    clip = halve(quad.reshape(ring, cols, quad.shape[1]), "yl", 0)
    own, probs, near, clip = lax.optimization_barrier((own, probs, near, clip))
    clip = exchange(clip.astype(jnp.bfloat16), "yh")
    own = own.reshape(row_count * SHARE, width)
    other = lax.ppermute(own, "c", SWAP)
    grad_rows = project_call(core_id, own, other, dout, near, seq_count)
    grad_rows, clip = lax.optimization_barrier((grad_rows, clip))
    heads_grad = exchange(grad_rows, SEQ)

    line, across = lax.axis_size("x"), lax.axis_size("zh")
    pieces = arrange_call(clip, line, across)
    pieces, heads_grad, probs = lax.optimization_barrier((pieces, heads_grad, probs))
    pieces = exchange(pieces, "x")
    local = grads_call(heads_qkv, heads_grad, probs)
    local, pieces = lax.optimization_barrier((local, pieces))

    pieces = jnp.sum(pieces.astype(jnp.float32), axis=0).reshape(across, 24, LANES)
    grad_new = jnp.zeros((24, LANES), jnp.float32)
    for turn in range(across):
        moves = [
            ((z * line + x) * 2 + c, (c * across + (z + turn) % across) * line + x)
            for z in range(across)
            for x in range(line)
            for c in range(2)
        ]
        grad_new = grad_new + lax.ppermute(at(pieces, (lax.axis_index("zh") + turn) % across), DP, moves)
    grad_new = grad_new[:rows, :cols]

    back = exchange(local, SEQ)
    dqkv = jnp.transpose(back, (3, 1, 0, 2)).reshape(tokens, 3, width)
    return (dqkv, grad_new, weight_new, moment_one, moment_two)


def solution(mesh):
    fine = Mesh(mesh.devices.reshape(4, 8, 2, 2, 4, 2), DP + SEQ)
    rows = P(DP + SEQ)
    square = P(DP, SEQ)
    return jax.shard_map(
        per_device,
        mesh=fine,
        in_specs=(rows, rows, rows, square, square, square, square),
        out_specs=(rows, square, square, square, square),
        check_vma=False,
    )
```
